128 devices in a mesh: frame: 4 (over x_lo, core), row: 32 (over z, y, x_hi).
Axes of the slice: x: 4 (x_hi: 2, x_lo: 2; x = x_hi * 2 + x_lo), y: 4, z: 4, core: 2. Of those that a mesh axis runs over, the one named last changes fastest.
Arguments:
- queries: bfloat16 [4, 256, 16, 1536], P('frame', 'row'), may hold values from -128 to 128
- keys: bfloat16 [4, 256, 16, 1536], P('frame', 'row'), may hold values from -6 to 6
- values: bfloat16 [4, 256, 16, 1536], P('frame', 'row'), may hold values from -6 to 6
- window_mask: int32 [4, 32, 2, 45], P('frame', 'row'), may hold values 0 or 1
- tile_valid: int32 [4, 32, 2], replicated, may hold values 0 or 1
- w_out: bfloat16 [1536, 3072], replicated, may hold values from -0.5 to 0.5
- gate: float32 [3072], replicated, may hold values from 0.5 to 4
Outputs:
- update: bfloat16 [4, 256, 16, 3072], P('frame', 'row')
The draws below stay inside these ranges and needn't reach their ends.
All inputs are finite; a program needn't handle non-finite values. No bound on the sum of `window_mask` on one device may be relied on, other than what follows from the above.
Results may differ from the reference program's by a relative error of at most 0.0053.
Values may be sent and summed in bfloat16 or wider, within the bound.
No kernel may reach another device: no remote copies, remote signals or barrier semaphores. Data moves between devices by JAX's collectives and lax.ppermute only.
A program may use at most 128 MiB of HBM per device.

```python
import math
import jax
import jax.numpy as jnp
from jax import lax

D = 3072
HEADS = 12
HD = 128
FR_TILE = 1
ROW_TILE = 8
COL_TILE = 8
OFFSETS = 45
WID = 16
FRAMES = 4
ROWS = 256
COL_TILES = 2
N_FRAME = 4
N_ROW = 32


def pair_draw(key):
    grid_shape = (FR_TILE * N_FRAME, ROW_TILE * N_ROW, WID, HEADS * HD)
    key_query = jax.random.fold_in(key, 101)
    key_keys = jax.random.fold_in(key, 202)
    query_base = 2.0 * jnp.clip(jax.random.normal(key_query, grid_shape, jnp.float32), -6.0, 6.0)
    key_base = jnp.clip(jax.random.normal(key_keys, grid_shape, jnp.float32), -6.0, 6.0)
    return (query_base, key_base)


def draw_queries(key, part):
    return pair_draw(key)[0].astype(jnp.bfloat16)


def draw_keys(key, part):
    return pair_draw(key)[1].astype(jnp.bfloat16)


def set_ends(entries, own_key, smallest, largest):
    index_at = [jax.random.randint(jax.random.fold_in(own_key, axis), (), 0, length) for axis, length in enumerate(entries.shape)]
    longest = entries.shape.index(max(entries.shape))
    neighbour = index_at[:longest] + [(index_at[longest] + 1) % entries.shape[longest]] + index_at[longest + 1:]
    return entries.at[tuple(index_at)].set(smallest).at[tuple(neighbour)].set(largest)


def levels(stream_key, shape, split, least, largest):
    gain, own = 1.0, jax.random.fold_in(stream_key, 6)
    for dim, shards_of in split:
        heights = jnp.exp(jax.random.uniform(jax.random.fold_in(own, dim), (shards_of,), jnp.float32, least / len(split), largest / len(split)))
        gain = gain * jnp.repeat(heights, shape[dim] // shards_of).reshape([-1 if axis == dim else 1 for axis in range(len(shape))])
    return gain


def bell_draw(key, extent, spread, bound, pieces=(), kind=jnp.bfloat16):
    factor_of = levels(key, extent, pieces, -0.22, 0.18) if pieces else 1.0
    values = jax.random.normal(key, extent, jnp.float32) * spread * factor_of
    return jnp.minimum(jnp.maximum(values, -bound), bound).astype(kind)


def setup_inputs(seed: int = 0) -> dict:
    splits = jax.random.split(jax.random.key(seed), 8)
    return {
        "queries": draw_queries(jax.random.fold_in(splits[7], 71), 0),
        "keys": draw_keys(jax.random.fold_in(splits[7], 71), 0),
        "values": bell_draw(splits[2], (FRAMES, ROWS, WID, HEADS * HD), 1.0, 6.0, ((0, 4), (1, 32))),
        "window_mask": set_ends((jax.random.randint(splits[3], (N_FRAME, N_ROW, COL_TILES, OFFSETS), 0, 4) < 3).astype(jnp.int32), jax.random.fold_in(splits[3], 1), 0, 1),
        "tile_valid": set_ends((jax.random.randint(splits[4], (N_FRAME, N_ROW, COL_TILES), 0, 6) < 5).astype(jnp.int32), jax.random.fold_in(splits[4], 1), 0, 1),
        "w_out": bell_draw(splits[5], (HEADS * HD, D), HD ** -0.5, 0.5),
        "gate": jnp.clip(jnp.exp(jax.random.uniform(splits[6], (D,), jnp.float32, math.log(0.5), math.log(4.0))), 0.5, 4.0),
    }


def tile_usage(offset_mask, tile_flags):
    col_tiles = offset_mask.shape[0]
    window_table = offset_mask.reshape(col_tiles, 3, 5, 3) == 1
    inside = tile_flags[:, :, 1:col_tiles + 1] == 1
    query_col = jnp.arange(col_tiles)[:, None]
    key_col = jnp.arange(col_tiles)[None, :]
    centre = (jnp.arange(3)[:, None] == 1) & (jnp.arange(5)[None, :] == 2)
    usable = jnp.zeros((col_tiles, 3, 5, col_tiles), dtype=bool)
    for shift_col in (-1, 0, 1):
        col_pair = key_col - query_col == shift_col
        allowed = window_table[:, :, :, shift_col + 1][:, :, :, None] & inside[None]
        if shift_col == 0:
            allowed = allowed | centre[None, :, :, None]
        usable = usable | col_pair[:, None, None, :] & allowed
    return usable

def attend_block(queries, key_ext, value_ext, usable, w_out, gate):
    frames, rows_here, columns, width = queries.shape
    col_tiles = usable.shape[0]
    tile_w = columns // col_tiles
    tok_count = frames * rows_here * columns
    key_count = key_ext.shape[0] * key_ext.shape[1] * columns
    key_mask = jnp.broadcast_to(usable.reshape(1, 1, col_tiles, 1, 3, 1, 5, 1, col_tiles, 1), (frames, rows_here, col_tiles, tile_w, 3, frames, 5, rows_here, col_tiles, tile_w)).reshape(tok_count, key_count)
    flat_query = queries.reshape(tok_count, width)
    flat_key = key_ext.reshape(key_count, width)
    flat_value = value_ext.reshape(key_count, width)
    score_scale = 1.0 / math.sqrt(HD)

    def one_head(head_id):
        start = (head_id * HD).astype(jnp.int32)
        query_head = lax.dynamic_slice_in_dim(flat_query, start, HD, 1)
        key_head = lax.dynamic_slice_in_dim(flat_key, start, HD, 1)
        value_head = lax.dynamic_slice_in_dim(flat_value, start, HD, 1)
        scores = jnp.dot(query_head, key_head.T, preferred_element_type=jnp.float32) * score_scale
        scores = jnp.where(key_mask, scores, -1e+30)
        highest = lax.optimization_barrier(jnp.max(scores, axis=1, keepdims=True))
        weights = jnp.where(key_mask, jnp.exp(scores - highest), 0.0)
        totals = lax.optimization_barrier(jnp.sum(weights, axis=1, keepdims=True))
        mixed = jnp.dot(weights.astype(jnp.bfloat16), value_head, preferred_element_type=jnp.float32)
        return mixed / totals
    head_outs = lax.map(one_head, jnp.arange(HEADS, dtype=jnp.int32))
    attention = head_outs.transpose(1, 0, 2).reshape(tok_count, width).astype(jnp.bfloat16)
    update = jnp.dot(attention, w_out, preferred_element_type=jnp.float32) * gate[None, :]
    return update.astype(jnp.bfloat16).reshape(frames, rows_here, columns, w_out.shape[1])

def reference(queries, keys, values, window_mask, tile_valid, w_out, gate):
    pad_spec = ((FR_TILE, FR_TILE), (2 * ROW_TILE, 2 * ROW_TILE), (0, 0), (0, 0))
    padded_keys = jnp.pad(keys, pad_spec)
    padded_values = jnp.pad(values, pad_spec)
    padded_flags = jnp.pad(tile_valid, ((1, 1), (2, 2), (1, 1)))
    col_tiles = WID // COL_TILE
    zero = jnp.int32(0)

    def one_block(block_id):
        block_id = block_id.astype(jnp.int32)
        frame_idx = (block_id // N_ROW).astype(jnp.int32)
        row_idx = (block_id % N_ROW).astype(jnp.int32)
        start_frame = (frame_idx * FR_TILE).astype(jnp.int32)
        start_row = (row_idx * ROW_TILE).astype(jnp.int32)
        query_block = lax.dynamic_slice(queries, (start_frame, start_row, zero, zero), (FR_TILE, ROW_TILE, WID, HEADS * HD))
        key_block = lax.dynamic_slice(padded_keys, (start_frame, start_row, zero, zero), (3 * FR_TILE, 5 * ROW_TILE, WID, HEADS * HD))
        value_block = lax.dynamic_slice(padded_values, (start_frame, start_row, zero, zero), (3 * FR_TILE, 5 * ROW_TILE, WID, HEADS * HD))
        tile_flags = lax.dynamic_slice(padded_flags, (frame_idx, row_idx, zero), (3, 5, col_tiles + 2))
        offset_mask = lax.dynamic_slice(window_mask, (frame_idx, row_idx, zero, zero), (1, 1, col_tiles, OFFSETS))[0, 0]
        usable = tile_usage(offset_mask, tile_flags)
        return attend_block(query_block, key_block, value_block, usable, w_out, gate)
    blocks = lax.map(one_block, jnp.arange(N_FRAME * N_ROW, dtype=jnp.int32))
    blocks = blocks.reshape(N_FRAME, N_ROW, FR_TILE, ROW_TILE, WID, D)
    return blocks.transpose(0, 2, 1, 3, 4, 5).reshape(N_FRAME * FR_TILE, N_ROW * ROW_TILE, WID, D)
```

```python
import math

import jax
import jax.numpy as jnp
from jax import lax
from jax.experimental import pallas as pl
from jax.experimental.pallas import tpu as pltpu
from jax.sharding import PartitionSpec as P

HEADS = 12
HD = 128
TOK = 128
LOG2E = 1.4426950408889634
SCALE = LOG2E / math.sqrt(HD)
NEG = -1e30


def row_sign(index):
    return 1 - 2 * (index % 2)


def row_pairs(count, step):
    pairs = [(i, i + step * row_sign(i)) for i in range(count)]
    return [(i, j) for i, j in pairs if 0 <= j < count]


def frame_move(value, step):
    count = lax.axis_size("frame")
    pairs = [(i, i + step) for i in range(count) if 0 <= i + step < count]
    return lax.ppermute(value, "frame", pairs)


def prep_kernel(frames, rows, mask_ref, valid_ref, pos_ref, q_ref, out_ref):
    f, r = pos_ref[0], pos_ref[1]
    sign = 1 - 2 * lax.rem(r, 2)
    lane = lax.broadcasted_iota(jnp.int32, (8, HD), 1)
    halves = []
    for c in range(2):
        block = jnp.zeros((8, HD), jnp.float32)
        for g in range(3):
            kf = f + (g - 1)
            for i, step in enumerate((0, 1, 2, -2, -1)):
                move = step * sign
                kr = r + move
                inside = (kf >= 0) & (kf < frames) & (kr >= 0) & (kr < rows)
                kf_in = jnp.clip(kf, 0, frames - 1)
                kr_in = jnp.clip(kr, 0, rows - 1)
                for kc in range(2):
                    if g == 1 and i == 0 and kc == c:
                        continue
                    offset = 15 * g + 3 * (move + 2) + (kc - c + 1)
                    usable = inside & (mask_ref[c, offset] == 1) & (valid_ref[kf_in, 2 * kr_in + kc] == 1)
                    bias = jnp.where(usable, 0.0, NEG)
                    block = jnp.where(lane == 10 * g + 2 * i + kc, bias, block)
        halves.append(block)
    both = jnp.concatenate(halves, 0)
    out_ref[:, : HEADS * HD] = q_ref[...]
    out_ref[:, HEADS * HD :] = jnp.concatenate([both] * (TOK // 16), 0).astype(jnp.bfloat16)


def attend_kernel(qp_ref, qo_ref, qn_ref, *refs):
    slots = (len(refs) - 5) // 2
    k_refs, v_refs = refs[:slots], refs[slots : 2 * slots]
    own_ref, own_stat_ref, prev_ref, next_ref, stat_ref = refs[2 * slots :]
    keys = slots * TOK
    width = HEADS * HD
    row = lax.broadcasted_iota(jnp.int32, (keys, HD), 0)
    lane = lax.broadcasted_iota(jnp.int32, (keys, HD), 1)
    kind = 2 * (row // TOK) + (row // 8) % 2
    key_aug = jnp.where((lane % 10 == kind) & (lane < 30), 1.0, 0.0).astype(jnp.bfloat16)
    qlane = lax.broadcasted_iota(jnp.int32, (TOK, HD), 1)
    augs = []
    for g, ref in ((2, qp_ref), (1, qo_ref), (0, qn_ref)):
        aug = ref[:, width:].astype(jnp.float32)
        augs.append(jnp.where((qlane >= 10 * g) & (qlane < 10 * g + 10), aug, 0.0))
    q_aug = jnp.concatenate(augs, 0).astype(jnp.bfloat16)
    ones = jnp.ones((keys, HD), jnp.bfloat16)
    slane = lax.broadcasted_iota(jnp.int32, (3 * TOK, HD), 1)
    stat_ref[...] = jnp.zeros_like(stat_ref)

    def head(h):
        at = pl.ds(pl.multiple_of(h * HD, HD), HD)
        q = jnp.concatenate([qp_ref[:, at], qo_ref[:, at], qn_ref[:, at]], 0)
        k = jnp.concatenate([ref[:, at] for ref in k_refs], 0)
        v = jnp.concatenate([ref[:, at] for ref in v_refs], 0)
        s = lax.dot_general(
            jnp.concatenate([q, q_aug], 1),
            jnp.concatenate([k, key_aug], 1),
            (((1,), (1,)), ((), ())),
            preferred_element_type=jnp.float32,
        )
        m = jnp.max(s, axis=1, keepdims=True)
        p = jnp.exp2((s - m) * SCALE).astype(jnp.bfloat16)
        both = jnp.dot(p, jnp.concatenate([v, ones], 1), preferred_element_type=jnp.float32)
        total = both[:, HD:]
        o = both[:, :HD] / total
        lse = m * SCALE + jnp.log2(total)
        hi = lse.astype(jnp.bfloat16).astype(jnp.float32)
        mid = (lse - hi).astype(jnp.bfloat16).astype(jnp.float32)
        low = lse - hi - mid
        stat = stat_ref[...]
        stat = jnp.where(slane == 3 * h, hi, stat)
        stat = jnp.where(slane == 3 * h + 1, mid, stat)
        stat_ref[...] = jnp.where(slane == 3 * h + 2, low, stat)
        prev_ref[:, at] = o[:TOK].astype(jnp.bfloat16)
        own_ref[:, at] = o[TOK : 2 * TOK]
        next_ref[:, at] = o[2 * TOK :].astype(jnp.bfloat16)

    def pair(h, carry):
        head(2 * h)
        head(2 * h + 1)
        return carry

    lax.fori_loop(0, HEADS // 2, pair, 0)
    prev_ref[:, width:] = stat_ref[:TOK].astype(jnp.bfloat16)
    own_stat_ref[...] = stat_ref[TOK : 2 * TOK].astype(jnp.bfloat16)
    next_ref[:, width:] = stat_ref[2 * TOK :].astype(jnp.bfloat16)


def project_kernel(frames, pos_ref, own_ref, own_stat_ref, prev_ref, next_ref, w_ref, gate_ref, out_ref, att_ref):
    width = HEADS * HD

    @pl.when(pl.program_id(0) == 0)
    def _():
        f = pos_ref[0]
        row = lax.broadcasted_iota(jnp.int32, (HD, width), 0)
        lane = lax.broadcasted_iota(jnp.int32, (HD, width), 1)
        spread = jnp.where(row // 3 == lane // HD, 1.0, 0.0).astype(jnp.bfloat16)

        def lse_of(stat):
            return jnp.dot(stat, spread, preferred_element_type=jnp.float32)

        lse_own = lse_of(own_stat_ref[...])
        lse_prev = jnp.where(f > 0, lse_of(prev_ref[:, width:]), NEG)
        lse_next = jnp.where(f < frames - 1, lse_of(next_ref[:, width:]), NEG)
        top = jnp.maximum(lse_own, jnp.maximum(lse_prev, lse_next))
        w_own = jnp.exp2(lse_own - top)
        w_prev = jnp.exp2(lse_prev - top)
        w_next = jnp.exp2(lse_next - top)
        mixed = (
            w_own * own_ref[...]
            + w_prev * prev_ref[:, :width].astype(jnp.float32)
            + w_next * next_ref[:, :width].astype(jnp.float32)
        )
        att_ref[...] = (mixed / (w_own + w_prev + w_next)).astype(jnp.bfloat16)

    update = jnp.dot(att_ref[...], w_ref[...], preferred_element_type=jnp.float32)
    out_ref[...] = (update * gate_ref[...]).astype(jnp.bfloat16)


def local(queries, keys, values, window_mask, tile_valid, w_out, gate):
    frames, rows = lax.axis_size("frame"), lax.axis_size("row")
    width = HEADS * HD
    depth = w_out.shape[1]
    vmem = pl.BlockSpec(memory_space=pltpu.VMEM)
    smem = pl.BlockSpec(memory_space=pltpu.SMEM)
    pos = jnp.stack([lax.axis_index("frame"), lax.axis_index("row")]).astype(jnp.int32)
    q = queries.reshape(TOK, width)
    k = keys.reshape(TOK, width)
    v = values.reshape(TOK, width)

    swap = row_pairs(rows, 1)
    far = [(j, i) for i, j in row_pairs(rows, 2)]
    near = row_pairs(rows, 2)
    k_a, v_a = [lax.ppermute(t, "row", far) for t in (k, v)]
    k_x, v_x = [lax.ppermute(t, "row", swap) for t in (k, v)]
    k_b, v_b = [lax.ppermute(t, "row", near) for t in (k, v)]
    q_ext = pl.pallas_call(
        lambda *refs: prep_kernel(frames, rows, *refs),
        out_shape=jax.ShapeDtypeStruct((TOK, width + HD), jnp.bfloat16),
        in_specs=[smem, smem, smem, vmem],
        out_specs=vmem,
    )(window_mask.reshape(2, 45), tile_valid.reshape(frames, 2 * rows), pos, q)
    q_prev = frame_move(q_ext, 1)
    q_next = frame_move(q_ext, -1)
    k_d = lax.ppermute(k_x, "row", near)
    v_d = lax.ppermute(v_a, "row", swap)

    ext = jax.ShapeDtypeStruct((TOK, width + HD), jnp.bfloat16)
    own, own_stat, for_prev, for_next = pl.pallas_call(
        attend_kernel,
        out_shape=(
            jax.ShapeDtypeStruct((TOK, width), jnp.float32),
            jax.ShapeDtypeStruct((TOK, HD), jnp.bfloat16),
            ext,
            ext,
        ),
        in_specs=[vmem] * 13,
        out_specs=[vmem] * 4,
        scratch_shapes=[pltpu.VMEM((3 * TOK, HD), jnp.float32)],
    )(q_prev, q_ext, q_next, k, k_x, k_a, k_b, k_d, v, v_x, v_a, v_b, v_d)
    from_next = frame_move(for_prev, -1)
    from_prev = frame_move(for_next, 1)

    block = 768
    out = pl.pallas_call(
        lambda *refs: project_kernel(frames, *refs),
        out_shape=jax.ShapeDtypeStruct((TOK, depth), jnp.bfloat16),
        grid=(depth // block,),
        in_specs=[smem, vmem, vmem, vmem, vmem,
                  pl.BlockSpec((width, block), lambda n: (0, n)),
                  pl.BlockSpec((1, block), lambda n: (0, n))],
        out_specs=pl.BlockSpec((TOK, block), lambda n: (0, n)),
        scratch_shapes=[pltpu.VMEM((TOK, width), jnp.bfloat16)],
    )(pos, own, own_stat, from_prev, from_next, w_out, gate.reshape(1, depth))
    return out.reshape(1, 8, 16, depth)


def solution(mesh):
    placed = (P("frame", "row", None, None),) * 4 + (P(), P(), P())
    return jax.shard_map(
        local, mesh=mesh, in_specs=placed, out_specs=P("frame", "row", None, None), check_vma=False
    )
```

```python
import math

import jax
import jax.numpy as jnp
from jax import lax
from jax.experimental import pallas as pl
from jax.experimental.pallas import tpu as pltpu
from jax.sharding import PartitionSpec as P


HEADS = 12
HD = 128
TOK = 128
WIDTH = HEADS * HD
LOG2E = 1.4426950408889634
SCALE = LOG2E / math.sqrt(HD)
NEG = -1e30
COUNTS = {"ext": 1, "own": 2, "state": 2, "none": 0}
STEPS = (0, 1, 2, -2, -1)
VMEM = pl.BlockSpec(memory_space=pltpu.VMEM)
SMEM = pl.BlockSpec(memory_space=pltpu.SMEM)
BLOCK = 512
LIMIT = 24 * 1024 * 1024


def row_sign(index):
    return 1 - 2 * (index % 2)


def row_pairs(count, step):
    pairs = [(i, i + step * row_sign(i)) for i in range(count)]
    return [(i, j) for i, j in pairs if 0 <= j < count]


def row_move(value, pairs):
    return lax.ppermute(value, "row", pairs)


def frame_swap(value, first):
    count = lax.axis_size("frame")
    pairs = []
    for i in range(first, count - 1, 2):
        pairs += [(i, i + 1), (i + 1, i)]
    return lax.ppermute(value, "frame", pairs)


def cross_swap(value):
    count, rows = lax.axis_size("frame"), lax.axis_size("row")
    pairs = []
    for i in range(1, count - 1, 2):
        for r in range(rows):
            pairs += [(i * rows + r, (i + 1) * rows + (r ^ 1)), ((i + 1) * rows + r, i * rows + (r ^ 1))]
    return lax.ppermute(value, ("frame", "row"), pairs)


def prep_kernel(frames, rows, mask_ref, valid_ref, q_ref, out_ref):
    f, r = lax.axis_index("frame"), lax.axis_index("row")
    sign = 1 - 2 * lax.rem(r, 2)
    lane = lax.broadcasted_iota(jnp.int32, (8, HD), 1)
    halves = []
    for c in range(2):
        block = jnp.zeros((8, HD), jnp.float32)
        for g in range(3):
            kf = f + (g - 1)
            for i, step in enumerate(STEPS):
                move = step * sign
                kr = r + move
                inside = (kf >= 0) & (kf < frames) & (kr >= 0) & (kr < rows)
                kf_in = jnp.clip(kf, 0, frames - 1)
                kr_in = jnp.clip(kr, 0, rows - 1)
                for kc in range(2):
                    if g == 1 and i == 0 and kc == c:
                        continue
                    offset = 15 * g + 3 * (move + 2) + (kc - c + 1)
                    usable = inside & (mask_ref[c, offset] == 1) & (valid_ref[kf_in, kc, kr_in] == 1)
                    bias = jnp.where(usable, 0.0, NEG)
                    block = jnp.where(lane == 10 * g + 2 * i + kc, bias, block)
        halves.append(block)
    both = jnp.concatenate(halves, 0)
    out_ref[:, :WIDTH] = q_ref[...]
    out_ref[:, WIDTH:] = jnp.concatenate([both] * (TOK // 16), 0).astype(jnp.bfloat16)


def lane_group(who):
    odd = lax.rem(lax.axis_index("frame"), 2)
    return {"own": 1, "even": 2 * odd, "odd": 2 - 2 * odd}[who]


def attend_kernel(whose, slots, parts, emits, has_state, together, *refs):
    refs = list(refs)
    n, rows, keys = len(slots), len(whose) * TOK, len(slots) * TOK
    q_refs = [refs.pop(0) for _ in whose]
    kv_refs = [[refs.pop(0) for _ in range(count)] for count in parts]
    old = [(refs.pop(0), refs.pop(0)) for _ in whose] if has_state else []
    outs = [[refs.pop(0) for _ in range(COUNTS[emit])] for emit in emits]
    row = lax.broadcasted_iota(jnp.int32, (TOK, HD), 0)
    lane = lax.broadcasted_iota(jnp.int32, (TOK, HD), 1)
    augs = []
    for ref, who in zip(q_refs, whose):
        low = 10 * lane_group(who)
        aug = ref[:, WIDTH:].astype(jnp.float32)
        augs.append(jnp.where((lane >= low) & (lane < low + 10), aug, 0.0))
    q_aug = jnp.concatenate(augs, 0).astype(jnp.bfloat16)
    col = (row // 8) % 2
    kinds = []
    for i in slots:
        match = (lane % 10 == 2 * i + col) & (lane < 30)
        kinds.append(jnp.where(match, 1.0, 0.0))
    key_aug = jnp.concatenate(kinds, 0).astype(jnp.bfloat16)
    ones = jnp.ones((keys, HD), jnp.bfloat16)

    def block(h, size=HD):
        return pl.ds(h * size, size) if isinstance(h, int) else pl.ds(pl.multiple_of(h * size, size), size)

    def tile(i, h, which):
        return kv_refs[i][0][which, :, block(h)] if parts[i] == 1 else kv_refs[i][which][:, block(h)]

    def head(h, stats):
        at, wide = block(h), block(h, 2 * HD)
        q = jnp.concatenate([ref[:, at] for ref in q_refs], 0)
        k = jnp.concatenate([tile(i, h, 0) for i in range(n)], 0)
        v = jnp.concatenate([tile(i, h, 1) for i in range(n)], 0)
        s = lax.dot_general(
            jnp.concatenate([q, q_aug], 1),
            jnp.concatenate([k, key_aug], 1),
            (((1,), (1,)), ((), ())),
            preferred_element_type=jnp.float32,
        )
        top = jnp.broadcast_to(jnp.max(s, axis=1, keepdims=True), (rows, HD))
        if has_state:
            was = jnp.concatenate([tops[:, at] for _, tops in old], 0)
            top = jnp.maximum(top, was)
            fade = jnp.exp2((was - top) * SCALE)
        p = jnp.exp2((s - jnp.concatenate([top] * n, 1)) * SCALE).astype(jnp.bfloat16)
        both = jnp.dot(p, jnp.concatenate([v, ones], 1), preferred_element_type=jnp.float32)
        if has_state:
            sums = jnp.concatenate([sums[:, wide] for sums, _ in old], 0)
            both = both + sums * jnp.concatenate([fade, fade], 1)
        new_stats = []
        for j, (emit, out, stat) in enumerate(zip(emits, outs, stats)):
            if emit == "none":
                new_stats.append(stat)
                continue
            mine = slice(j * TOK, (j + 1) * TOK)
            if emit == "state":
                out[0][:, wide] = both[mine]
                out[1][:, at] = top[mine]
                new_stats.append(stat)
                continue
            total = both[mine, HD:]
            o = both[mine, :HD] / total
            lse = top[mine] * SCALE + jnp.log2(total)
            if emit == "own":
                out[0][:, at] = o
                out[1][:, at] = lse
                new_stats.append(stat)
                continue
            hi = lse.astype(jnp.bfloat16).astype(jnp.float32)
            mid = (lse - hi).astype(jnp.bfloat16).astype(jnp.float32)
            low = lse - hi - mid
            stat = jnp.where(lane == 3 * h, hi, stat)
            stat = jnp.where(lane == 3 * h + 1, mid, stat)
            new_stats.append(jnp.where(lane == 3 * h + 2, low, stat))
            out[0][:, at] = o.astype(jnp.bfloat16)
        return tuple(new_stats)

    def group(i, stats):
        for j in range(together):
            stats = head(together * i + j, stats)
        return stats

    stats = tuple(jnp.zeros((TOK, HD), jnp.float32) if emit == "ext" else jnp.int32(0) for emit in emits)
    if together == HEADS:
        stats = group(0, stats)
    else:
        stats = lax.fori_loop(0, HEADS // together, group, stats)
    for emit, out, stat in zip(emits, outs, stats):
        if emit == "ext":
            out[0][:, WIDTH:] = stat.astype(jnp.bfloat16)


def attend(queries, tiles, state, emits, together=HEADS):
    whose, slots = tuple(queries), tuple(tiles)
    rows = len(whose) * TOK
    parts = tuple(len(tile) for tile in tiles.values())
    args = list(queries.values()) + [t for tile in tiles.values() for t in tile]
    if state is not None:
        args += [t for who in whose for t in state[who]]
    shapes = []
    for emit in emits:
        if emit == "none":
            continue
        if emit == "ext":
            shapes += [jax.ShapeDtypeStruct((TOK, WIDTH + HD), jnp.bfloat16)]
        else:
            first = 2 * WIDTH if emit == "state" else WIDTH
            shapes += [jax.ShapeDtypeStruct((TOK, first), jnp.float32), jax.ShapeDtypeStruct((TOK, WIDTH), jnp.float32)]
    outs = pl.pallas_call(
        lambda *refs: attend_kernel(whose, slots, parts, emits, state is not None, together, *refs),
        out_shape=shapes,
        in_specs=[VMEM] * len(args),
        out_specs=[VMEM] * len(shapes),
        compiler_params=pltpu.CompilerParams(vmem_limit_bytes=LIMIT),
        cost_estimate=pl.CostEstimate(
            flops=HEADS * rows * len(slots) * TOK * HD * 16, bytes_accessed=4 << 20, transcendentals=HEADS * rows * len(slots) * TOK
        ),
    )(*args)
    outs = list(outs)
    given = [outs.pop(0) if emit == "ext" else tuple(outs.pop(0) for _ in range(COUNTS[emit])) for emit in emits]
    return dict(zip(whose, given))


def merged(own_ref, own_lse_ref, back):
    row = lax.broadcasted_iota(jnp.int32, (HD, WIDTH), 0)
    lane = lax.broadcasted_iota(jnp.int32, (HD, WIDTH), 1)
    spread = jnp.where(row // 3 == lane // HD, 1.0, 0.0).astype(jnp.bfloat16)
    lses = [own_lse_ref[...]]
    for ref, there in back:
        lse = jnp.dot(ref[:, WIDTH:], spread, preferred_element_type=jnp.float32)
        lses.append(jnp.where(there, lse, NEG))
    top = lses[0]
    for lse in lses[1:]:
        top = jnp.maximum(top, lse)
    shares = [jnp.exp2(lse - top) for lse in lses]
    mixed = shares[0] * own_ref[...]
    whole = shares[0]
    for (ref, _), share in zip(back, shares[1:]):
        mixed = mixed + share * ref[:, :WIDTH].astype(jnp.float32)
        whole = whole + share
    return mixed / whole, top, whole


def pair_there(frames, who):
    f = lax.axis_index("frame")
    odd = lax.rem(f, 2)
    return (f - odd + 1) < frames if who == "even" else (f > 0) & (f + odd < frames)


def merge_kernel(frames, whose, own_ref, own_lse_ref, *refs):
    back = [(ref, pair_there(frames, who)) for ref, who in zip(refs, whose)]
    out_ref, lse_ref = refs[len(whose) :]
    mixed, top, whole = merged(own_ref, own_lse_ref, back)
    out_ref[...] = mixed
    lse_ref[...] = top + jnp.log2(whole)


def project_kernel(frames, whose, own_ref, own_lse_ref, *refs):
    back = [(ref, pair_there(frames, who)) for ref, who in zip(refs, whose)]
    w_ref, gate_ref, out_ref, att_ref, block_ref, sems = refs[len(whose) :]
    att_ref[...] = merged(own_ref, own_lse_ref, back)[0].astype(jnp.bfloat16)
    copies = []
    for n in range(out_ref.shape[1] // BLOCK):
        at = pl.ds(n * BLOCK, BLOCK)
        update = jnp.dot(att_ref[...], w_ref[:, at], preferred_element_type=jnp.float32)
        block_ref[n] = (update * gate_ref[:, at]).astype(jnp.bfloat16)
        copies.append(pltpu.make_async_copy(block_ref.at[n], out_ref.at[:, at], sems.at[n]))
        copies[-1].start()
    for copy in copies:
        copy.wait()


def merge(own, own_lse, back):
    frames, whose = lax.axis_size("frame"), tuple(back)
    return pl.pallas_call(
        lambda *refs: merge_kernel(frames, whose, *refs),
        out_shape=[jax.ShapeDtypeStruct(own.shape, jnp.float32)] * 2,
        in_specs=[VMEM] * (2 + len(whose)),
        out_specs=[VMEM] * 2,
        compiler_params=pltpu.CompilerParams(vmem_limit_bytes=LIMIT),
        cost_estimate=pl.CostEstimate(flops=1 << 24, bytes_accessed=1 << 20, transcendentals=1 << 19),
    )(own, own_lse, *back.values())


def local(queries, keys, values, window_mask, tile_valid, w_out, gate):
    frames, rows = lax.axis_size("frame"), lax.axis_size("row")
    depth = w_out.shape[1]
    q = queries.reshape(TOK, WIDTH)
    k = keys.reshape(TOK, WIDTH)
    v = values.reshape(TOK, WIDTH)

    swap = row_pairs(rows, 1)
    near = row_pairs(rows, 2)
    far = [(j, i) for i, j in near]
    x_k = row_move(k, swap)
    kv = jnp.stack([k, v])
    a = row_move(kv, far)
    b = row_move(kv, near)
    q_ext = pl.pallas_call(
        lambda *refs: prep_kernel(frames, rows, *refs),
        out_shape=jax.ShapeDtypeStruct((TOK, WIDTH + HD), jnp.bfloat16),
        in_specs=[SMEM, SMEM, VMEM],
        out_specs=VMEM,
        name="prep",
        compiler_params=pltpu.CompilerParams(vmem_limit_bytes=LIMIT),
        cost_estimate=pl.CostEstimate(flops=1 << 20, bytes_accessed=1 << 20, transcendentals=0),
    )(window_mask.reshape(window_mask.shape[2:]), tile_valid.transpose(0, 2, 1), q)
    q_odd = frame_swap(q_ext, 1)
    q_cross = cross_swap(q_ext)
    q_even = frame_swap(q_ext, 0)
    x = (x_k, row_move(v, swap))
    d = (row_move(x_k, near), row_move(a[1], swap))

    early = {0: (kv,), 1: x, 2: (a,), 3: (b,)}
    cross = attend({"odd": q_cross}, {4: (a,)}, None, ("ext",))["odd"]
    cross = cross_swap(cross)
    own_x = {i: early[i] for i in (0, 1)}
    a_b = {i: early[i] for i in (2, 3)}
    pair = {"even": q_even, "own": q_ext}
    state = attend(pair, own_x, None, ("state", "state"))
    odd = attend({"odd": q_odd, "own": q_ext}, early, None, ("ext", "none"))["odd"]
    state = attend(pair, a_b, state, ("state", "state"))
    odd = frame_swap(odd, 1)
    last = attend(pair, {4: d}, state, ("ext", "own"))
    even = frame_swap(last["even"], 0)
    own, own_lse = last["own"]

    own = merge(own, own_lse, {"even": even, "odd": cross})
    out = pl.pallas_call(
        lambda *refs: project_kernel(frames, ("odd",), *refs),
        out_shape=jax.ShapeDtypeStruct((TOK, depth), jnp.bfloat16),
        in_specs=[VMEM] * 5,
        out_specs=pl.BlockSpec(memory_space=pl.ANY),
        scratch_shapes=[
            pltpu.VMEM((TOK, WIDTH), jnp.bfloat16),
            pltpu.VMEM((depth // BLOCK, TOK, BLOCK), jnp.bfloat16),
            pltpu.SemaphoreType.DMA((depth // BLOCK,)),
        ],
        name="project",
        compiler_params=pltpu.CompilerParams(vmem_limit_bytes=LIMIT),
        cost_estimate=pl.CostEstimate(flops=2 * TOK * WIDTH * depth, bytes_accessed=1 << 20, transcendentals=0),
    )(*own, odd, w_out, gate.reshape(1, depth))
    return out.reshape(1, 8, 16, depth)


def solution(mesh):
    placed = (P("frame", "row", None, None),) * 4 + (P(), P(), P())

    return jax.shard_map(local, mesh=mesh, in_specs=placed, out_specs=P("frame", "row", None, None), check_vma=False)
```
